32 devices in a mesh: dp: 2 (over y), seq: 8 (over z, x), head: 2 (over core).
Axes of the slice: x: 2, y: 2, z: 4, core: 2. Of those that a mesh axis runs over, the one named last changes fastest.
Arguments:
- tokens: bfloat16 [2, 2, 1024, 2048], P(None, 'dp', 'seq'), may hold values from -6 to 6
- norm_gain: float32 [2048], replicated, may hold values from 0.5 to 1.5
- w_gate_in: bfloat16 [2048, 4096], P(('dp', 'seq'), 'head'), may hold values from -0.125 to 0.125
- w_x_in: bfloat16 [2048, 4096], P(('dp', 'seq'), 'head'), may hold values from -0.125 to 0.125
- w_bc_in: bfloat16 [2048, 256], P(('dp', 'seq')), may hold values from -0.125 to 0.125
- w_dt_in: bfloat16 [2048, 64], P(('dp', 'seq'), 'head'), may hold values from -0.0625 to 0.0625
- conv_x_w: float32 [4, 4096], P(None, 'head'), may hold values from -3 to 3
- conv_x_b: float32 [4096], P('head'), may hold values from -3 to 3
- conv_bc_w: float32 [4, 256], replicated, may hold values from -3 to 3
- conv_bc_b: float32 [256], replicated, may hold values from -3 to 3
- dt_bias: float32 [64], P('head'), may hold values from -7 to -2
- a_log: float32 [64], P('head'), may hold values from 0 to 1.5
- d_skip: float32 [64], P('head'), may hold values from 0.5 to 1.5
- gate_gain: float32 [4096], P('head'), may hold values from 0.5 to 1.5
- w_out: bfloat16 [4096, 2048], P('head', ('dp', 'seq')), may hold values from -0.09375 to 0.09375
- prefix_len: int32 [2, 2], P(None, 'dp'), may hold values from 102 to 1024, as said below
- cotangent: bfloat16 [2, 2, 1024, 2048], P(None, 'dp', 'seq'), may hold values from -6 to 6
Outputs:
- result: bfloat16 [2, 2, 1024, 2048], P(None, 'dp', 'seq')
- grad_tokens: float32 [2, 2, 1024, 2048], P(None, 'dp', 'seq')
- grad_norm_gain: float32 [2048], replicated
- grad_w_gate_in: float32 [2048, 4096], P(('dp', 'seq'), 'head')
- grad_w_x_in: float32 [2048, 4096], P(('dp', 'seq'), 'head')
- grad_w_bc_in: float32 [2048, 256], P(('dp', 'seq'))
- grad_w_dt_in: float32 [2048, 64], P(('dp', 'seq'), 'head')
- grad_conv_x_w: float32 [4, 4096], P(None, 'head')
- grad_conv_x_b: float32 [4096], P('head')
- grad_conv_bc_w: float32 [4, 256], replicated
- grad_conv_bc_b: float32 [256], replicated
- grad_dt_bias: float32 [64], P('head')
- grad_a_log: float32 [64], P('head')
- grad_d_skip: float32 [64], P('head')
- grad_gate_gain: float32 [4096], P('head')
- grad_w_out: float32 [4096, 2048], P('head', ('dp', 'seq'))
The draws below stay inside these ranges and needn't reach their ends.
Inputs may be any that keep to these rules, and one draw needn't show every extreme that they name: Tokens before a sequence's prefix_len mix both ways; some sequence has exactly 1024 and some exactly 102.
All inputs are finite; a program needn't handle non-finite values.
Results may differ from the reference program's by a relative error of at most 0.012.
Values may be sent and summed in bfloat16 or wider, within the bound.
A program may use at most 256 MiB of HBM per device.

```python
import math
import jax
import jax.numpy as jnp
from jax import lax

D = 2048
DI = 4096
HEADS = 64
STATE = 128
CONV = 4
MICRO = 2
SEQ_LEN = 1024
SEQS = 2


def draw_prefix_len(key, part):
    lowest = SEQ_LEN // 10
    highest = SEQ_LEN
    subkeys = jax.random.split(key, 3)
    values = jax.random.randint(subkeys[0], (MICRO, SEQS), lowest, highest + 1)
    flattened = values.reshape(-1)
    slot_count = flattened.shape[0]
    top_slot = jax.random.randint(subkeys[1], (), 0, slot_count)
    low_slot = (top_slot + 1 + jax.random.randint(subkeys[2], (), 0, slot_count - 1)) % slot_count
    flattened = flattened.at[top_slot].set(highest).at[low_slot].set(lowest)
    return flattened.reshape(MICRO, SEQS).astype(jnp.int32)


def shard_levels(rng, dims, cuts, smallest, high):
    factor_of, own = 1.0, jax.random.fold_in(rng, 6)
    for axis_at, shards_of in cuts:
        draws = jnp.exp(jax.random.uniform(jax.random.fold_in(own, axis_at), (shards_of,), jnp.float32, smallest / len(cuts), high / len(cuts)))
        factor_of = factor_of * jnp.repeat(draws, dims[axis_at] // shards_of).reshape([-1 if axis == axis_at else 1 for axis in range(len(dims))])
    return factor_of


def scatter_about(key, shape, width, most, cuts=(), kind=jnp.bfloat16):
    gain = shard_levels(key, shape, cuts, -0.22, 0.18) if cuts else 1.0
    drawn = jax.random.normal(key, shape, jnp.float32) * width * gain
    return jnp.minimum(jnp.maximum(drawn, -most), most).astype(kind)


def setup_inputs(seed: int = 0) -> dict:
    keys = jax.random.split(jax.random.key(seed), 18)
    return {
        "tokens": scatter_about(keys[0], (MICRO, SEQS, SEQ_LEN, D), 1.0, 6.0, ((1, 2), (2, 8))),
        "norm_gain": jnp.clip(1.0 + 0.1 * jax.random.normal(keys[1], (D,), jnp.float32), 0.5, 1.5),
        "w_gate_in": scatter_about(keys[2], (D, DI), D ** -0.5, 0.125, ((0, 16), (1, 2))),
        "w_x_in": scatter_about(keys[3], (D, DI), D ** -0.5, 0.125, ((0, 16), (1, 2))),
        "w_bc_in": scatter_about(keys[4], (D, 2 * STATE), D ** -0.5, 0.125, ((0, 16),)),
        "w_dt_in": scatter_about(keys[5], (D, HEADS), (4 * D) ** -0.5, 0.0625, ((0, 16), (1, 2))),
        "conv_x_w": scatter_about(keys[6], (CONV, DI), CONV ** -0.5, 3.0, ((1, 2),), jnp.float32),
        "conv_x_b": scatter_about(keys[7], (DI,), 0.5, 3.0, ((0, 2),), jnp.float32),
        "conv_bc_w": scatter_about(keys[8], (CONV, 2 * STATE), CONV ** -0.5, 3.0, (), jnp.float32),
        "conv_bc_b": scatter_about(keys[9], (2 * STATE,), 0.5, 3.0, (), jnp.float32),
        "dt_bias": jnp.clip(-7.0 + 5.0 * jax.random.uniform(keys[10], (HEADS,), jnp.float32) ** shard_levels(keys[10], (HEADS,), ((0, 2),), -0.2, 0.2), -7.0, -2.0),
        "a_log": jnp.clip(1.5 * jax.random.uniform(keys[11], (HEADS,), jnp.float32) ** shard_levels(keys[11], (HEADS,), ((0, 2),), -0.2, 0.2), 0.0, 1.5),
        "d_skip": jnp.clip(0.5 + 1.0 * jax.random.uniform(keys[12], (HEADS,), jnp.float32) ** shard_levels(keys[12], (HEADS,), ((0, 2),), -0.2, 0.2), 0.5, 1.5),
        "gate_gain": jnp.clip(1.0 + 0.1 * jax.random.normal(keys[13], (DI,), jnp.float32), 0.5, 1.5),
        "w_out": scatter_about(keys[14], (DI, D), DI ** -0.5, 0.09375, ((0, 2), (1, 16))),
        "prefix_len": draw_prefix_len(jax.random.fold_in(keys[17], 71), 0),
        "cotangent": scatter_about(keys[16], (MICRO, SEQS, SEQ_LEN, D), 1.0, 6.0, ((1, 2), (2, 8))),
    }


EPSILON = 1e-05
HIGHEST = lax.Precision.HIGHEST

@jax.custom_vjp
def low(v):
    return lax.optimization_barrier(v.astype(jnp.bfloat16)).astype(jnp.float32)

@jax.custom_vjp
def low_back(v):
    return v

def low_keep(v):
    return (low(v), None)

def low_pass(kept, grad):
    return (grad,)

def back_keep(v):
    return (v, None)

def back_low(kept, grad):
    return (low(grad),)
low.defvjp(low_keep, low_pass)
low_back.defvjp(back_keep, back_low)

def exact_product(left_side, right_side):
    return jnp.dot(left_side, right_side, precision=HIGHEST, preferred_element_type=jnp.float32)

def rms_scale(token_rows, gain_vector):
    return token_rows * lax.rsqrt(lax.optimization_barrier(jnp.mean(token_rows * token_rows, axis=-1, keepdims=True)) + EPSILON) * gain_vector

def causal_conv(signal, kernel, bias_vector):
    margin = kernel.shape[0] - 1
    length = signal.shape[0]
    padded = jnp.concatenate([jnp.zeros((margin, signal.shape[1]), jnp.float32), signal], axis=0)
    summed = bias_vector + jnp.zeros_like(signal)
    for offset in range(kernel.shape[0]):
        summed = summed + kernel[offset] * padded[offset:offset + length]
    return summed

def ssd_sequence(values, b_input, c_output, steps_dt, rates, prefix):
    length, head_count, head_width = values.shape
    block_size = math.gcd(length, 256)
    block_count = length // block_size
    weighted = (values * steps_dt[:, :, None]).reshape(block_count, block_size, head_count, head_width)
    cumulated = jnp.cumsum(rates.reshape(block_count, block_size, head_count), axis=1)
    final_cum = cumulated[:, -1, :]
    b_blocks = b_input.reshape(block_count, block_size, -1)
    c_blocks = c_output.reshape(block_count, block_size, -1)
    places = jnp.arange(length, dtype=jnp.int32).reshape(block_count, block_size)
    carried = jnp.exp(final_cum[:, None, :] - cumulated)
    ends_state = jnp.einsum('kth,kthp,ktn->khpn', carried, weighted, b_blocks, precision=HIGHEST)
    opening = jnp.where((places < prefix)[:, :, None], jnp.exp(cumulated), 0.0)
    back_state = jnp.einsum('kth,kthp,ktn->khpn', opening, weighted, b_blocks, precision=HIGHEST)
    decay_rate = jnp.exp(final_cum)

    def advance(carried_state, element):
        factor, state_add = element
        return (carried_state * factor[:, None, None] + state_add, carried_state)
    zero_state = jnp.zeros(ends_state.shape[1:], jnp.float32)
    _, state_in = lax.scan(advance, zero_state, (decay_rate, ends_state))
    _, back_in = lax.scan(advance, zero_state, (decay_rate, back_state), reverse=True)

    def block_output(element):
        cum_block, end_block, b_block, c_block, w_block, place_block, incoming, returning = element
        scores = jnp.dot(c_block, b_block.T, precision=HIGHEST, preferred_element_type=jnp.float32)
        spread = cum_block[:, None, :] - cum_block[None, :, :]
        behind_mask = (place_block[:, None] >= place_block[None, :])[:, :, None]
        ahead_mask = ((place_block[:, None] < place_block[None, :]) & (place_block[None, :] < prefix))[:, :, None]
        masked = jnp.where(behind_mask, jnp.exp(jnp.where(behind_mask, spread, 0.0)), 0.0) + jnp.where(ahead_mask, jnp.exp(jnp.where(ahead_mask, -spread, 0.0)), 0.0)
        result = jnp.einsum('tsh,shp->thp', scores[:, :, None] * masked, w_block, precision=HIGHEST)
        result = result + jnp.exp(cum_block)[:, :, None] * jnp.einsum('tn,hpn->thp', c_block, incoming, precision=HIGHEST)
        result = result + jnp.exp(end_block[None, :] - cum_block)[:, :, None] * jnp.einsum('tn,hpn->thp', c_block, returning, precision=HIGHEST)
        return result
    outputs = lax.map(jax.checkpoint(block_output), (cumulated, final_cum, b_blocks, c_blocks, weighted, places, state_in, back_in))
    return outputs.reshape(length, head_count, head_width)

def sequence_forward(token_rows, prefix, parameters):
    norm_gain, w_gate_in, w_x_in, w_bc_in, w_dt_in, conv_x_w, conv_x_b, conv_bc_w, conv_bc_b, dt_bias, a_log, d_skip, gate_gain, w_out = parameters
    length = token_rows.shape[0]
    state_size = w_bc_in.shape[1] // 2
    normed = low(rms_scale(token_rows, norm_gain))
    gate_low = low_back(low(exact_product(normed, w_gate_in)))
    inner_low = low_back(low(exact_product(normed, w_x_in)))
    bc_low = low_back(low(exact_product(normed, w_bc_in)))
    dt_raw = low_back(low(exact_product(normed, w_dt_in)))
    inner_act = jax.nn.silu(causal_conv(inner_low, conv_x_w, conv_x_b))
    bc_act = jax.nn.silu(causal_conv(bc_low, conv_bc_w, conv_bc_b))
    head_count = dt_raw.shape[1]
    values = inner_act.reshape(length, head_count, -1)
    b_input = bc_act[:, :state_size]
    c_output = bc_act[:, state_size:]
    steps_dt = jax.nn.softplus(dt_raw + dt_bias)
    rates = steps_dt * -jnp.exp(a_log)
    mixed_out = ssd_sequence(values, b_input, c_output, steps_dt, rates, prefix) + d_skip[:, None] * values
    gated_out = mixed_out.reshape(length, -1) * jax.nn.silu(gate_low)
    scaled = low(rms_scale(gated_out, gate_gain))
    return token_rows + exact_product(scaled, w_out)

def reference(tokens, norm_gain, w_gate_in, w_x_in, w_bc_in, w_dt_in, conv_x_w, conv_x_b, conv_bc_w, conv_bc_b, dt_bias, a_log, d_skip, gate_gain, w_out, prefix_len, cotangent):
    parameters = tuple((weight.astype(jnp.float32) for weight in (norm_gain, w_gate_in, w_x_in, w_bc_in, w_dt_in, conv_x_w, conv_x_b, conv_bc_w, conv_bc_b, dt_bias, a_log, d_skip, gate_gain, w_out)))
    micro_count, seq_count, length, model_width = tokens.shape
    flat_tokens = tokens.astype(jnp.float32).reshape(micro_count * seq_count, length, model_width)
    flat_prefix = prefix_len.reshape(micro_count * seq_count)

    def forward(token_all, weights):
        per_sequence = jax.checkpoint(lambda element: sequence_forward(element[0], element[1], weights))
        return lax.map(per_sequence, (token_all, flat_prefix))
    result, pullback = jax.vjp(forward, flat_tokens, parameters)
    grad_flat, grad_params = pullback(cotangent.astype(jnp.float32).reshape(micro_count * seq_count, length, model_width))
    return (result.reshape(tokens.shape).astype(jnp.bfloat16), grad_flat.reshape(tokens.shape), grad_params[0], grad_params[1], grad_params[2], grad_params[3], grad_params[4], grad_params[5], grad_params[6], grad_params[7], grad_params[8], grad_params[9], grad_params[10], grad_params[11], grad_params[12], grad_params[13])
```

```python
import jax
import jax.numpy as jnp
from jax import lax
from jax.sharding import PartitionSpec as P

EPSILON = 1e-05
HIGHEST = lax.Precision.HIGHEST
BF16 = jnp.bfloat16
F32 = jnp.float32
CHUNK = 128


def dot_f32(a, b):
    return jnp.dot(a, b, preferred_element_type=F32)


def causal_conv(signal, kernel, bias):
    margin = kernel.shape[0] - 1
    length = signal.shape[1]
    padded = jnp.pad(signal, ((0, 0), (margin, 0), (0, 0)))
    summed = bias + jnp.zeros_like(signal)
    for offset in range(kernel.shape[0]):
        summed = summed + kernel[offset] * padded[:, offset : offset + length]
    return summed


def mixer(prefix, inner, bc, dt_raw, conv_x_w, conv_x_b, conv_bc_w, conv_bc_b, dt_bias, a_log, d_skip):
    seqs, length, width = inner.shape
    heads = dt_raw.shape[-1]
    state = bc.shape[-1] // 2
    chunk = CHUNK
    count = length // chunk
    values = jax.nn.silu(causal_conv(inner, conv_x_w, conv_x_b))
    active = jax.nn.silu(causal_conv(bc, conv_bc_w, conv_bc_b))
    values = values.reshape(seqs, count, chunk, heads, width // heads)
    b_in = active[..., :state].reshape(seqs, count, chunk, state)
    c_out = active[..., state:].reshape(seqs, count, chunk, state)
    dt = jax.nn.softplus(dt_raw + dt_bias).reshape(seqs, count, chunk, heads)
    cum = jnp.cumsum(dt * -jnp.exp(a_log), axis=2)
    end = cum[:, :, -1:, :]
    places = jnp.arange(length, dtype=jnp.int32).reshape(count, chunk)
    inside = (places[None] < prefix[:, None, None])[..., None]
    weighted = values * dt[..., None]
    ends_state = jnp.einsum("skth,skthp,sktn->skhpn", jnp.exp(end - cum), weighted, b_in, precision=HIGHEST)
    back_state = jnp.einsum(
        "skth,skthp,sktn->skhpn", jnp.where(inside, jnp.exp(cum), 0.0), weighted, b_in, precision=HIGHEST
    )
    decay = jnp.exp(end[:, :, 0])[..., None, None]
    zero = jnp.zeros_like(ends_state[:, 0])
    state_in, back_in = [zero], [zero]
    for k in range(count - 1):
        state_in.append(state_in[-1] * decay[:, k] + ends_state[:, k])
        back_in.append(back_in[-1] * decay[:, count - 1 - k] + back_state[:, count - 1 - k])
    state_in = jnp.stack(state_in, axis=1)
    back_in = jnp.stack(back_in[::-1], axis=1)
    scores = jnp.einsum("sktn,skun->sktu", c_out, b_in, precision=HIGHEST)
    spread = cum[:, :, :, None, :] - cum[:, :, None, :, :]
    behind = (places[:, :, None] >= places[:, None, :])[None, ..., None]
    ahead = ((places[:, :, None] < places[:, None, :])[None] & (places[None, :, None, :] < prefix[:, None, None, None]))[
        ..., None
    ]
    masked = jnp.where(behind, jnp.exp(jnp.where(behind, spread, 0.0)), 0.0) + jnp.where(
        ahead, jnp.exp(jnp.where(ahead, -spread, 0.0)), 0.0
    )
    out = jnp.einsum("sktuh,skuhp->skthp", scores[..., None] * masked, weighted, precision=HIGHEST)
    out = out + jnp.exp(cum)[..., None] * jnp.einsum("sktn,skhpn->skthp", c_out, state_in, precision=HIGHEST)
    out = out + jnp.exp(end - cum)[..., None] * jnp.einsum("sktn,skhpn->skthp", c_out, back_in, precision=HIGHEST)
    out = out + d_skip[:, None] * values
    return out.reshape(seqs, length, width)


def body(
    tokens, norm_gain, w_gate_in, w_x_in, w_bc_in, w_dt_in, conv_x_w, conv_x_b, conv_bc_w, conv_bc_b,
    dt_bias, a_log, d_skip, gate_gain, w_out, prefix_len, cotangent,
):
    dp, sq, hd = lax.axis_size("dp"), lax.axis_size("seq"), lax.axis_size("head")
    me_seq, me_head = lax.axis_index("seq"), lax.axis_index("head")
    micro, seqs, span, model = tokens.shape
    group = micro * seqs
    length = span * sq
    rows_here = group * span
    own_rows = rows_here // hd
    half = w_x_in.shape[1]
    width = half // sq
    heads = w_dt_in.shape[1] // sq
    full_inner = half * hd
    prefix = prefix_len.reshape(group)
    everyone = ("seq", "head")

    def mine(x):
        return lax.dynamic_slice_in_dim(x.reshape(rows_here, model), me_head * own_rows, own_rows, 0)

    def to_sequences(x):
        return x.reshape(sq, group, span, -1).transpose(1, 0, 2, 3).reshape(group, length, -1)

    def from_sequences(x):
        return x.reshape(group, sq, span, -1).transpose(1, 0, 2, 3).reshape(sq * rows_here, -1)

    def rms(x, gain):
        return x * lax.rsqrt(jnp.mean(x * x, axis=-1, keepdims=True) + EPSILON) * gain

    my_tokens = mine(tokens).astype(F32)
    my_cot = mine(cotangent)
    normed_own = rms(my_tokens, norm_gain).astype(BF16)
    normed = lax.all_gather(normed_own, everyone, axis=0, tiled=True)

    def columns(w):
        return lax.all_gather(
            lax.all_to_all(w, "seq", split_axis=1, concat_axis=0, tiled=True), "dp", axis=0, tiled=True
        )

    wg = columns(w_gate_in)
    wx = columns(w_x_in)
    wd = lax.dynamic_slice_in_dim(
        lax.all_gather(w_dt_in, ("dp", "seq"), axis=0, tiled=True), me_seq * heads, heads, 1
    )
    wb = lax.all_gather(w_bc_in, ("dp", "seq"), axis=0, tiled=True)
    wo = lax.all_gather(
        lax.all_to_all(w_out, "seq", split_axis=0, concat_axis=1, tiled=True), "dp", axis=1, tiled=True
    )
    cot = lax.all_gather(my_cot, everyone, axis=0, tiled=True)

    def part(x, size, axis):
        return lax.dynamic_slice_in_dim(x, me_seq * size, size, axis)

    cxw, cxb = part(conv_x_w, width, 1), part(conv_x_b, width, 0)
    dtb, alog, dsk = part(dt_bias, heads, 0), part(a_log, heads, 0), part(d_skip, heads, 0)
    gain = part(gate_gain, width, 0)

    def project(w):
        return to_sequences(dot_f32(normed, w).astype(BF16)).astype(F32)

    gate, inner, bc, dt_raw = project(wg), project(wx), project(wb), project(wd)
    mixed, pull = jax.vjp(
        lambda *a: mixer(prefix, *a), inner, bc, dt_raw, cxw, cxb, conv_bc_w, conv_bc_b, dtb, alog, dsk
    )
    sig = jax.nn.sigmoid(gate)
    act = gate * sig
    gated = mixed * act
    grad_scaled = to_sequences(
        jnp.einsum("rd,kd->rk", cot, wo, preferred_element_type=F32)
    )
    gs = grad_scaled * gain
    sums = lax.psum(
        jnp.stack([jnp.sum(gated * gated, axis=-1), jnp.sum(gs * gated, axis=-1)]), everyone
    )
    scale = lax.rsqrt(sums[0][..., None] / full_inner + EPSILON)
    unit = gated * scale
    scaled = from_sequences((unit * gain).astype(BF16))
    branch = lax.psum_scatter(
        dot_f32(scaled, wo).astype(BF16), everyone, scatter_dimension=0, tiled=True
    )
    result_own = (my_tokens + branch.astype(F32)).astype(BF16)
    grad_gain = jnp.sum(grad_scaled * unit, axis=(0, 1))
    grad_wo = jnp.einsum("rk,rd->kd", scaled, cot, preferred_element_type=F32)
    grad_gated = gs * scale - gated * (scale * scale * scale * (sums[1][..., None] / full_inner))
    grad_mixed = grad_gated * act
    grad_gate = grad_gated * mixed * (sig * (1.0 + gate * (1.0 - sig)))
    d_inner, d_bc, d_dt, d_cxw, d_cxb, d_cbw, d_cbb, d_dtb, d_alog, d_dsk = pull(grad_mixed)
    gg = from_sequences(grad_gate.astype(BF16))
    gx = from_sequences(d_inner.astype(BF16))
    gd = from_sequences(d_dt.astype(BF16))
    gb_own = lax.psum_scatter(from_sequences(d_bc), everyone, scatter_dimension=0, tiled=True).astype(BF16)

    def inward(g, w):
        return jnp.einsum("rc,kc->rk", g, w, preferred_element_type=F32)

    def weight_grad(n, g):
        return jnp.einsum("rk,rc->kc", n, g, preferred_element_type=F32)

    part_normed = inward(gg, wg) + inward(gx, wx) + inward(gd, wd)
    grad_normed = lax.psum_scatter(
        part_normed.astype(BF16), everyone, scatter_dimension=0, tiled=True
    ).astype(F32) + inward(gb_own, wb)
    _, pull_norm = jax.vjp(rms, my_tokens, norm_gain)
    grad_rows, grad_norm = pull_norm(grad_normed)
    grad_own = my_cot.astype(F32) + grad_rows

    def home(g):
        return lax.all_to_all(
            lax.psum_scatter(g.astype(BF16), "dp", scatter_dimension=0, tiled=True),
            "seq", split_axis=0, concat_axis=1, tiled=True,
        ).astype(F32)

    g_gate, g_x = home(weight_grad(normed, gg)), home(weight_grad(normed, gx))
    g_dt = lax.all_to_all(
        lax.psum_scatter(weight_grad(normed, gd), "dp", scatter_dimension=0, tiled=True),
        "seq", split_axis=0, concat_axis=1, tiled=True,
    )
    g_bc = lax.psum_scatter(
        lax.psum(weight_grad(normed_own, gb_own), "head"), ("dp", "seq"), scatter_dimension=0, tiled=True
    )
    g_out = lax.all_to_all(
        lax.psum_scatter(grad_wo.astype(BF16), "dp", scatter_dimension=1, tiled=True),
        "seq", split_axis=1, concat_axis=0, tiled=True,
    ).astype(F32)

    def whole(x):
        return lax.all_gather(x, "head", axis=0, tiled=True).reshape(micro, seqs, span, model)

    small = lax.psum((d_cxw, d_cxb, d_dtb, d_alog, d_dsk, grad_gain), "dp")
    small = [lax.all_gather(a, "seq", axis=a.ndim - 1, tiled=True) for a in small]
    grad_norm, d_cbw, d_cbb = lax.psum((grad_norm, d_cbw, d_cbb), ("dp", "seq", "head"))
    return (
        whole(result_own), whole(grad_own), grad_norm, g_gate, g_x, g_bc, g_dt,
        small[0], small[1], d_cbw, d_cbb, small[2], small[3], small[4], small[5], g_out,
    )


def solution(mesh):
    rows = P(("dp", "seq"), "head")
    tok = P(None, "dp", "seq", None)
    return jax.shard_map(
        body,
        mesh=mesh,
        in_specs=(
            tok, P(), rows, rows, P(("dp", "seq"), None), rows, P(None, "head"), P("head"), P(), P(),
            P("head"), P("head"), P("head"), P("head"), P("head", ("dp", "seq")), P(None, "dp"), tok,
        ),
        out_specs=(
            tok, tok, P(), rows, rows, P(("dp", "seq"), None), rows, P(None, "head"), P("head"), P(), P(),
            P("head"), P("head"), P("head"), P("head"), P("head", ("dp", "seq")),
        ),
        check_vma=False,
    )
```

```python
import functools
import jax
import jax.numpy as jnp
from jax import lax
from jax.experimental import pallas as pl
from jax.experimental.pallas import tpu as pltpu

from jax.sharding import PartitionSpec as P

EPSILON = 1e-05
BF16 = jnp.bfloat16
F32 = jnp.float32
NN = (((1,), (0,)), ((), ()))
NT = (((1,), (1,)), ((), ()))
TN = (((0,), (0,)), ((), ()))


def mm(a, b, dims=NN):
    return lax.dot_general(a.astype(BF16), b.astype(BF16), dims, preferred_element_type=F32)


def pieces(a, count):
    out = []
    for _ in range(count):
        top = a.astype(BF16)
        out.append(top)
        a = a - top.astype(F32)
    return out


def mm_left(exact, a, count, dims=NN):
    return sum(mm(exact, piece, dims) for piece in pieces(a, count))


def mm_right(a, exact, count, dims=NN):
    return sum(mm(piece, exact, dims) for piece in pieces(a, count))


def sigmoid(x):
    return 1.0 / (1.0 + jnp.exp(-x))


def window(cur, before):
    return jnp.concatenate([before, cur], axis=0)


def column_sum(x):
    return jnp.sum(x, axis=0, keepdims=True)


def iota(shape, axis):
    return lax.broadcasted_iota(jnp.int32, shape, axis)


def one_hot(cond):
    return jnp.where(cond, 1.0, 0.0).astype(BF16)


def conv_window(p_ref, k, lo, hi):
    span = p_ref.shape[2]
    cur = p_ref[k, 0, :, lo:hi].astype(F32)
    prev = p_ref[jnp.maximum(k - 1, 0), 0, span - 16 :, lo:hi].astype(F32)[8:]
    return window(cur, jnp.where(k > 0, prev, 0.0))


def taps(win, span, j):
    return win[5 + j : 5 + j + span]


def conv(win, span, w_ref, b_ref):
    acc = b_ref[...] + w_ref[3:4, :] * taps(win, span, 3)
    for j in range(3):
        acc = acc + w_ref[j : j + 1, :] * taps(win, span, j)
    return acc


def chunk_masks(span, k, prefix):
    t, s = iota((span, span), 0), iota((span, span), 1)
    return t, s, (s <= t) | (s + k * span < prefix)


def forward_kernel(
    heads, state, prefix_ref, p_ref, gs_ref, cxw, cxb, cbw, cbb, dtb, nega, dsk, gain,
    xc_ref, bcc_ref, dt_ref, cum_ref, mixed_ref, sin_ref, rin_ref, sums_ref, s_scr, r_scr,
):
    count, _, span, _ = p_ref.shape
    width = cxw.shape[1]
    head_width = width // heads
    prefix = prefix_ref[pl.program_id(0)]
    expand = one_hot(iota((128, width), 0) == iota((128, width), 1) // head_width)
    tri = one_hot(iota((span, span), 1) <= iota((span, span), 0))
    row = iota((span, 1), 0)

    s_scr[...] = jnp.zeros_like(s_scr)
    r_scr[...] = jnp.zeros_like(r_scr)

    def ascend(k, carry):
        xc = conv(conv_window(p_ref, k, width, 2 * width), span, cxw, cxb)
        bcc = conv(conv_window(p_ref, k, 2 * width, 2 * width + 2 * state), span, cbw, cbb)
        xc_ref[k, 0] = xc
        bcc_ref[k, 0] = bcc
        v = xc * sigmoid(xc)
        raw = mm(p_ref[k, 0, :, 2 * width + 2 * state :], expand) + dtb[...]
        dt = jnp.maximum(raw, 0.0) + jnp.log1p(jnp.exp(-jnp.abs(raw)))
        cum = mm_left(tri, dt * nega[...], 3)
        dt_ref[k, 0] = dt
        cum_ref[k, 0] = cum
        b = bcc[:, :state] * sigmoid(bcc[:, :state])
        end = cum[span - 1 :, :]
        state_in = s_scr[...]
        sin_ref[k, 0] = state_in
        s_scr[...] = jnp.exp(end) * state_in + mm(b, jnp.exp(end - cum) * (dt * v), TN)
        return carry

    lax.fori_loop(0, count, ascend, 0)

    def descend(step, carry):
        k = count - 1 - step
        xc, bcc = xc_ref[k, 0], bcc_ref[k, 0]
        dt, cum = dt_ref[k, 0], cum_ref[k, 0]
        v = xc * sigmoid(xc)
        bc = bcc * sigmoid(bcc)
        b, c = bc[:, :state].astype(BF16), bc[:, state:].astype(BF16)
        end = cum[span - 1 :, :]
        w = dt * v
        t, s, mask = chunk_masks(span, k, prefix)
        scores = jnp.where(mask, mm(c, b, NT), 0.0)
        cum_t = cum.T
        lane_head = iota((span, width), 1) // head_width
        wb = w.astype(BF16)
        y = dsk[...] * v
        for h in range(heads):
            at = h * head_width
            decay = jnp.exp(-jnp.abs(cum[:, at : at + 1] - cum_t[at : at + 1, :]))
            y = y + jnp.where(lane_head == h, mm(scores * decay, wb), 0.0)
        back = r_scr[...]
        rin_ref[k, 0] = back
        y = y + jnp.exp(cum) * mm(c, sin_ref[k, 0]) + jnp.exp(end - cum) * mm(c, back)
        mixed_ref[k, 0] = y
        inside = row + k * span < prefix
        r_scr[...] = jnp.exp(end) * back + mm(b, jnp.where(inside, jnp.exp(cum) * w, 0.0), TN)
        gate = p_ref[k, 0, :, :width].astype(F32)
        gated = y * (gate * sigmoid(gate))
        ones = jnp.ones((8, width), BF16)
        square = mm_left(ones, gated * gated, 2, NT)
        cross = mm_left(ones, gated * (gs_ref[k, 0] * gain[...]), 2, NT)
        sums_ref[k, 0] = jnp.where(iota((8, span), 0) == 0, square, cross)
        return carry

    lax.fori_loop(0, count, descend, 0)


def backward_kernel(
    heads, state, full_inner, prefix_ref, p_ref, gs_ref, xc_ref, bcc_ref, dt_ref, cum_ref, mixed_ref, sin_ref,
    rin_ref, tot_ref, cxw, cxb, cbw, cbb, dtb, nega, dsk, gain,
    g_ref, scaled_ref, small_ref, smallbc_ref, dm_scr, j_scr, h_scr, nx_scr, nb_scr, jrun_scr,
):
    count, _, span, _ = p_ref.shape
    width = cxw.shape[1]
    head_width = width // heads
    prefix = prefix_ref[pl.program_id(0)]
    lane = iota((span, width), 1)
    lane_head = lane // head_width
    expand = one_hot(iota((128, width), 0) == iota((128, width), 1) // head_width)
    pick = one_hot(iota((width, 128), 0) == iota((width, 128), 1) * head_width)
    same_head = one_hot(iota((width, width), 0) // head_width == iota((width, width), 1) // head_width)
    later = one_hot(iota((span, span), 1) >= iota((span, span), 0))
    row = iota((span, 1), 0)

    @pl.when(pl.program_id(0) == 0)
    def _():
        small_ref[...] = jnp.zeros_like(small_ref)
        smallbc_ref[...] = jnp.zeros_like(smallbc_ref)

    for ref in (h_scr, nx_scr, nb_scr, jrun_scr):
        ref[...] = jnp.zeros_like(ref)

    def ascend(k, carry):
        tot = tot_ref[k, 0].T
        mean_sq = tot[:, 0:1] * (1.0 / full_inner)
        mean_x = tot[:, 1:2] * (1.0 / full_inner)
        scale = lax.rsqrt(mean_sq + EPSILON)
        gate = p_ref[k, 0, :, :width].astype(F32)
        sig = sigmoid(gate)
        act = gate * sig
        mixed = mixed_ref[k, 0]
        gated = mixed * act
        grad_scaled = gs_ref[k, 0]
        unit = gated * scale
        scaled_ref[k, 0] = (unit * gain[...]).astype(BF16)
        small_ref[5:6, :] += column_sum(grad_scaled * unit)
        dgated = grad_scaled * gain[...] * scale - unit * (scale * scale * mean_x)
        g_ref[k, 0, :, :width] = (dgated * mixed * (sig * (1.0 + gate * (1.0 - sig)))).astype(BF16)
        dm = dgated * act
        dm_scr[k] = dm
        cum = cum_ref[k, 0]
        end = cum[span - 1 :, :]
        cc = bcc_ref[k, 0, :, state:]
        c = cc * sigmoid(cc)
        jrun = jrun_scr[...]
        j_scr[k] = jrun
        jrun_scr[...] = jnp.exp(end) * jrun + mm(c, jnp.exp(end - cum) * dm, TN)
        return carry

    lax.fori_loop(0, count, ascend, 0)

    def descend(step, carry):
        k = count - 1 - step
        xc, bcc = xc_ref[k, 0], bcc_ref[k, 0]
        dt, cum, dm = dt_ref[k, 0], cum_ref[k, 0], dm_scr[k]
        xsig = sigmoid(xc)
        v = xc * xsig
        bsig = sigmoid(bcc)
        bc = bcc * bsig
        b, c = bc[:, :state].astype(BF16), bc[:, state:].astype(BF16)
        end = cum[span - 1 :, :]
        w = dt * v
        wb = w.astype(BF16)
        dmb = dm.astype(BF16)
        t, s, mask = chunk_masks(span, k, prefix)
        scores = jnp.where(mask, mm(c, b, NT), 0.0)
        side = jnp.where(t > s, 1.0, jnp.where(t < s, -1.0, 0.0))
        cum_t = cum.T
        dscore = jnp.zeros((span, span), F32)
        dw = jnp.zeros((span, width), F32)
        z = jnp.zeros((span, width), F32)
        for h in range(heads):
            at = h * head_width
            decay = jnp.exp(-jnp.abs(cum[:, at : at + 1] - cum_t[at : at + 1, :]))
            weight = scores * decay
            dm_h = jnp.where(lane_head == h, dmb, jnp.zeros_like(dmb))
            dweight = mm(dm_h, wb, NT)
            dw = dw + mm(weight, dm_h, TN)
            dscore = dscore + decay * dweight
            q = weight * dweight * side
            diff = jnp.sum(q - q.T, axis=1, keepdims=True)
            z = z + jnp.where(lane == at, diff, 0.0)
        dscore = jnp.where(mask, dscore, 0.0).astype(BF16)
        inside = row + k * span < prefix
        grow = jnp.exp(cum)
        fall = jnp.exp(end - cum)
        grow_in = jnp.where(inside, grow, 0.0)
        whole = jnp.exp(end)
        state_in, back_in = sin_ref[k, 0], rin_ref[k, 0]
        hgrad, jgrad = h_scr[...], j_scr[k]
        front = dm * grow
        rear = dm * fall
        wf = w * fall
        wg = w * grow_in
        bh, bj = mm(b, hgrad), mm(b, jgrad)
        out_b = rear * mm(c, back_in)
        src_f = wf * bh
        z = z + front * mm(c, state_in) - out_b - src_f + wg * bj
        edge = column_sum(out_b + src_f) + whole * column_sum(hgrad * state_in + jgrad * back_in)
        dw = dw + fall * bh + grow_in * bj
        dc = mm(dscore, b) + mm(front, state_in, NT) + mm(rear, back_in, NT)
        db = mm(dscore, c, TN) + mm(wf, hgrad, NT) + mm(wg, jgrad, NT)
        h_scr[...] = whole * hgrad + mm(c, front, TN)
        drate = mm_right(mm_left(later, z, 2) + edge, same_head, 2)
        raw = mm(p_ref[k, 0, :, 2 * width + 2 * state :], expand) + dtb[...]
        draw = (mm_right(v * dw, same_head, 2) + drate * nega[...]) * sigmoid(raw)
        small_ref[6:7, :] += column_sum(draw)
        small_ref[7:8, :] += column_sum(drate * (dt * nega[...]))
        small_ref[8:9, :] += column_sum(dm * v)
        g_ref[k, 0, :, 2 * width + 2 * state :] = mm(draw, pick).astype(BF16)
        dxc = (dt * dw + dsk[...] * dm) * (xsig * (1.0 + xc * (1.0 - xsig)))
        dbc = jnp.concatenate([db, dc], axis=1) * (bsig * (1.0 + bcc * (1.0 - bsig)))
        for grad, nref, sref, wref, lo, hi in (
            (dxc, nx_scr, small_ref, cxw, width, 2 * width),
            (dbc, nb_scr, smallbc_ref, cbw, 2 * width, 2 * width + 2 * state),
        ):
            win = conv_window(p_ref, k, lo, hi)
            for j in range(4):
                sref[j : j + 1, :] += column_sum(grad * taps(win, span, j))
            sref[4:5, :] += column_sum(grad)
            ext = jnp.concatenate([grad, nref[...]], axis=0)
            nref[...] = grad[:8]
            back = wref[3:4, :] * grad
            for j in range(3):
                back = back + wref[j : j + 1, :] * ext[3 - j : 3 - j + span]
            g_ref[k, 0, :, lo:hi] = back.astype(BF16)
        return carry

    lax.fori_loop(0, count, descend, 0)


def group_block(shape):
    return pl.BlockSpec((shape[0], 1) + tuple(shape[2:]), lambda g: (0, g, 0, 0))


def whole_block(a):
    return pl.BlockSpec(a.shape, lambda g: (0,) * a.ndim)


def ssd_forward(heads, state, prefix, p, gs, params):
    count, group, span, _ = p.shape
    width = params[0].shape[1]
    outs = [
        (count, group, span, width), (count, group, span, 2 * state), (count, group, span, width),
        (count, group, span, width), (count, group, span, width), (count, group, state, width),
        (count, group, state, width), (count, group, 8, span),
    ]
    return pl.pallas_call(
        functools.partial(forward_kernel, heads, state),
        grid=(group,),
        in_specs=[pl.BlockSpec(memory_space=pltpu.SMEM), group_block(p.shape), group_block(gs.shape)]
        + [whole_block(a) for a in params],
        out_specs=[group_block(o) for o in outs],
        out_shape=[jax.ShapeDtypeStruct(o, F32) for o in outs],
        scratch_shapes=[pltpu.VMEM((state, width), F32)] * 2,
        compiler_params=pltpu.CompilerParams(vmem_limit_bytes=56 << 20),
    )(prefix, p, gs, *params)


def ssd_backward(heads, state, full_inner, prefix, p, gs, saved, totals, params):
    count, group, span, cols = p.shape
    width = params[0].shape[1]
    ins = (p, gs) + tuple(saved) + (totals,)
    return pl.pallas_call(
        functools.partial(backward_kernel, heads, state, full_inner),
        grid=(group,),
        in_specs=[pl.BlockSpec(memory_space=pltpu.SMEM)]
        + [group_block(a.shape) for a in ins]
        + [whole_block(a) for a in params],
        out_specs=[
            group_block(p.shape), group_block((count, group, span, width)),
            pl.BlockSpec((16, width), lambda g: (0, 0)), pl.BlockSpec((8, 2 * state), lambda g: (0, 0)),
        ],
        out_shape=[
            jax.ShapeDtypeStruct(p.shape, BF16), jax.ShapeDtypeStruct((count, group, span, width), BF16),
            jax.ShapeDtypeStruct((16, width), F32), jax.ShapeDtypeStruct((8, 2 * state), F32),
        ],
        scratch_shapes=[
            pltpu.VMEM((count, span, width), F32), pltpu.VMEM((count, state, width), F32),
            pltpu.VMEM((state, width), F32), pltpu.VMEM((8, width), F32), pltpu.VMEM((8, 2 * state), F32),
            pltpu.VMEM((state, width), F32),
        ],
        compiler_params=pltpu.CompilerParams(vmem_limit_bytes=60 << 20),
    )(prefix, *ins, *params)


def rms(x, gain):
    return x * lax.rsqrt(jnp.mean(x * x, axis=-1, keepdims=True) + EPSILON) * gain


def body(
    tokens, norm_gain, w_gate_in, w_x_in, w_bc_in, w_dt_in, conv_x_w, conv_x_b, conv_bc_w, conv_bc_b,
    dt_bias, a_log, d_skip, gate_gain, w_out, prefix_len, cotangent,
):
    sq, hd = lax.axis_size("seq"), lax.axis_size("head")
    me_seq, me_head = lax.axis_index("seq"), lax.axis_index("head")
    micro, seqs, span, model = tokens.shape
    group = micro * seqs
    rows_here = group * span
    own_rows = rows_here // hd
    half = w_x_in.shape[1]
    width = half // sq
    heads = w_dt_in.shape[1] // sq
    state = w_bc_in.shape[1] // 2
    full_inner = half * hd
    prefix = prefix_len.reshape(group)
    everyone = ("seq", "head")

    def mine(x):
        return lax.dynamic_slice_in_dim(x.reshape(rows_here, model), me_head * own_rows, own_rows, 0)

    def blocks(x):
        return x.reshape(sq, group, span, -1)

    my_tokens = mine(tokens).astype(F32)
    my_cot = mine(cotangent)
    normed = lax.all_gather(rms(my_tokens, norm_gain).astype(BF16), everyone, axis=0, tiled=True)

    def columns(w):
        return lax.all_gather(
            lax.all_to_all(w, "seq", split_axis=1, concat_axis=0, tiled=True), "dp", axis=0, tiled=True
        )

    wd = lax.dynamic_slice_in_dim(
        lax.all_gather(w_dt_in, ("dp", "seq"), axis=0, tiled=True), me_seq * heads, heads, 1
    )
    wb = lax.all_gather(w_bc_in, ("dp", "seq"), axis=0, tiled=True)
    wcat = jnp.concatenate(
        [columns(w_gate_in), columns(w_x_in), wb, jnp.pad(wd, ((0, 0), (0, 128 - heads)))], axis=1
    )
    wo = lax.all_gather(
        lax.all_to_all(w_out, "seq", split_axis=0, concat_axis=1, tiled=True), "dp", axis=1, tiled=True
    )
    cot = lax.all_gather(my_cot, everyone, axis=0, tiled=True)

    def part(x, size, axis):
        return lax.dynamic_slice_in_dim(x, me_seq * size, size, axis)

    def spread(x):
        return jnp.repeat(part(x, heads, 0), width // heads)[None]

    params = (
        part(conv_x_w, width, 1), part(conv_x_b, width, 0)[None], conv_bc_w, conv_bc_b[None],
        spread(dt_bias), spread(-jnp.exp(a_log)), spread(d_skip), part(gate_gain, width, 0)[None],
    )
    p = blocks(jnp.dot(normed, wcat, preferred_element_type=F32).astype(BF16))
    gs = blocks(jnp.einsum("rd,kd->rk", cot, wo, preferred_element_type=F32))
    *saved, sums = ssd_forward(heads, state, prefix, p, gs, params)
    totals = lax.psum(sums, everyone)
    g, scaled, small, smallbc = ssd_backward(heads, state, full_inner, prefix, p, gs, saved, totals, params)
    g = g.reshape(sq * rows_here, -1)
    scaled = scaled.reshape(sq * rows_here, width)
    branch = lax.psum_scatter(
        jnp.dot(scaled, wo, preferred_element_type=F32).astype(BF16), everyone, scatter_dimension=0, tiled=True
    )
    result_own = (my_tokens + branch.astype(F32)).astype(BF16)
    part_normed = jnp.einsum("rc,kc->rk", g, wcat, preferred_element_type=F32)
    grad_normed = lax.psum_scatter(
        part_normed.astype(BF16), everyone, scatter_dimension=0, tiled=True
    ).astype(F32)
    gw = jnp.einsum("rk,rc->kc", normed, g, preferred_element_type=F32)
    g_wo = jnp.einsum("rk,rd->kd", scaled, cot, preferred_element_type=F32)
    grad_norm = jnp.sum(gw * wcat.astype(F32), axis=1) / norm_gain
    _, pull_norm = jax.vjp(lambda x: rms(x, norm_gain), my_tokens)
    grad_own = my_cot.astype(F32) + pull_norm(grad_normed)[0]

    def home(x):
        return lax.all_to_all(
            lax.psum_scatter(x, "dp", scatter_dimension=0, tiled=True),
            "seq", split_axis=0, concat_axis=1, tiled=True,
        )

    g_gate, g_x = (home(gw[:, at : at + width].astype(BF16)).astype(F32) for at in (0, width))
    g_dt = home(gw[:, 2 * width + 2 * state :][:, :heads])
    g_bc = lax.psum_scatter(
        lax.psum(gw[:, 2 * width : 2 * width + 2 * state], "head"), ("dp", "seq"), scatter_dimension=0, tiled=True
    )
    g_out = lax.all_to_all(
        lax.psum_scatter(g_wo.astype(BF16), "dp", scatter_dimension=1, tiled=True),
        "seq", split_axis=1, concat_axis=0, tiled=True,
    ).astype(F32)

    def whole(x):
        return lax.all_gather(x, "head", axis=0, tiled=True).reshape(micro, seqs, span, model)

    def per_head(x):
        return x.reshape(heads, width // heads)

    small = lax.all_gather(lax.psum(small, "dp"), "seq", axis=1, tiled=True)
    s_norm, s_bc = lax.psum((grad_norm, smallbc), ("dp", "seq", "head"))
    by_head = small.reshape(16, sq * heads, width // heads)
    return (
        whole(result_own), whole(grad_own), s_norm, g_gate, g_x, g_bc, g_dt,
        small[:4], small[4], s_bc[:4], s_bc[4], by_head[6, :, 0], by_head[7, :, 0], by_head[8].sum(-1), small[5], g_out,
    )


def solution(mesh):
    rows = P(("dp", "seq"), "head")
    tok = P(None, "dp", "seq", None)
    return jax.shard_map(
        body,
        mesh=mesh,
        in_specs=(
            tok, P(), rows, rows, P(("dp", "seq"), None), rows, P(None, "head"), P("head"), P(), P(),
            P("head"), P("head"), P("head"), P("head"), P("head", ("dp", "seq")), P(None, "dp"), tok,
        ),
        out_specs=(
            tok, tok, P(), rows, rows, P(("dp", "seq"), None), rows, P(None, "head"), P("head"), P(), P(),
            P("head"), P("head"), P("head"), P("head"), P("head", ("dp", "seq")),
        ),
        check_vma=False,
    )
```

```python
import functools
import jax
import jax.numpy as jnp
from jax import lax
from jax.experimental import pallas as pl
from jax.experimental.pallas import tpu as pltpu

from jax.sharding import PartitionSpec as P

EPSILON = 1e-05
BF16 = jnp.bfloat16
F32 = jnp.float32
NN = (((1,), (0,)), ((), ()))
NT = (((1,), (1,)), ((), ()))
TN = (((0,), (0,)), ((), ()))


def mm(a, b, dims=NN):
    return lax.dot_general(a.astype(BF16), b.astype(BF16), dims, preferred_element_type=F32)


def pieces(a, count):
    out = []
    for _ in range(count):
        top = a.astype(BF16)
        out.append(top)
        a = a - top.astype(F32)
    return out


def mm_left(exact, a, count, dims=NN):
    return sum(mm(exact, piece, dims) for piece in pieces(a, count))


def mm_right(a, exact, count, dims=NN):
    return sum(mm(piece, exact, dims) for piece in pieces(a, count))


def sigmoid(x):
    return 1.0 / (1.0 + jnp.exp(-x))


def window(cur, before):
    return jnp.concatenate([before, cur], axis=0)


def column_sum(x):
    return jnp.sum(x, axis=0, keepdims=True)


def iota(shape, axis):
    return lax.broadcasted_iota(jnp.int32, shape, axis)


def one_hot(cond):
    return jnp.where(cond, 1.0, 0.0).astype(BF16)


def column(row):
    return jnp.broadcast_to(row, (8, row.shape[1])).T[:, 0:1]


def conv_window(p_ref, k, lo, hi):
    span = p_ref.shape[2]
    cur = p_ref[k, 0, :, lo:hi].astype(F32)
    prev = p_ref[jnp.maximum(k - 1, 0), 0, span - 16 :, lo:hi].astype(F32)[8:]
    return window(cur, jnp.where(k > 0, prev, 0.0))


def taps(win, span, j):
    return win[5 + j : 5 + j + span]


def conv(win, span, w_ref, b_ref):
    acc = b_ref[...] + w_ref[3:4, :] * taps(win, span, 3)
    for j in range(3):
        acc = acc + w_ref[j : j + 1, :] * taps(win, span, j)
    return acc


def chunk_masks(span, k, prefix):
    t, s = iota((span, span), 0), iota((span, span), 1)
    return t, s, (s <= t) | (s + k * span < prefix)


def forward_kernel(
    heads, state, prefix_ref, p_ref, gs_ref, cxw, cxb, cbw, cbb, dtb, nega, dsk, gain,
    xc_ref, bcc_ref, dt_ref, cum_ref, mixed_ref, sin_ref, rin_ref, sums_ref, s_scr, r_scr,
):
    count, _, span, _ = p_ref.shape
    width = cxw.shape[1]
    head_width = width // heads
    prefix = prefix_ref[pl.program_id(0)]
    expand = one_hot(iota((128, width), 0) == iota((128, width), 1) // head_width)
    tri = one_hot(iota((span, span), 1) <= iota((span, span), 0))
    row = iota((span, 1), 0)

    s_scr[...] = jnp.zeros_like(s_scr)
    r_scr[...] = jnp.zeros_like(r_scr)

    def ascend(k, carry):
        xc = conv(conv_window(p_ref, k, width, 2 * width), span, cxw, cxb)
        bcc = conv(conv_window(p_ref, k, 2 * width, 2 * width + 2 * state), span, cbw, cbb)
        xc_ref[k, 0] = xc
        bcc_ref[k, 0] = bcc
        v = xc * sigmoid(xc)
        raw = mm(p_ref[k, 0, :, 2 * width + 2 * state :], expand) + dtb[...]
        dt = jnp.maximum(raw, 0.0) + jnp.log1p(jnp.exp(-jnp.abs(raw)))
        cum = mm_left(tri, dt * nega[...], 3)
        dt_ref[k, 0] = dt
        cum_ref[k, 0] = cum
        b = bcc[:, :state] * sigmoid(bcc[:, :state])
        end = cum[span - 1 :, :]
        state_in = s_scr[...]
        sin_ref[k, 0] = state_in
        s_scr[...] = jnp.exp(end) * state_in + mm(b, jnp.exp(end - cum) * (dt * v), TN)
        return carry

    lax.fori_loop(0, count, ascend, 0)

    def descend(step, carry):
        k = count - 1 - step
        xc, bcc = xc_ref[k, 0], bcc_ref[k, 0]
        dt, cum = dt_ref[k, 0], cum_ref[k, 0]
        v = xc * sigmoid(xc)
        bc = bcc * sigmoid(bcc)
        b, c = bc[:, :state].astype(BF16), bc[:, state:].astype(BF16)
        end = cum[span - 1 :, :]
        w = dt * v
        t, s, mask = chunk_masks(span, k, prefix)
        scores = jnp.where(mask, mm(c, b, NT), 0.0)
        cum_t = cum.T
        lane_head = iota((span, width), 1) // head_width
        wb = w.astype(BF16)
        y = dsk[...] * v
        for h in range(heads):
            at = h * head_width
            decay = jnp.exp(-jnp.abs(cum[:, at : at + 1] - cum_t[at : at + 1, :]))
            y = y + jnp.where(lane_head == h, mm(scores * decay, wb), 0.0)
        back = r_scr[...]
        rin_ref[k, 0] = back
        y = y + jnp.exp(cum) * mm(c, sin_ref[k, 0]) + jnp.exp(end - cum) * mm(c, back)
        mixed_ref[k, 0] = y
        inside = row + k * span < prefix
        r_scr[...] = jnp.exp(end) * back + mm(b, jnp.where(inside, jnp.exp(cum) * w, 0.0), TN)
        gate = p_ref[k, 0, :, :width].astype(F32)
        gated = y * (gate * sigmoid(gate))
        ones = jnp.ones((8, width), BF16)
        square = mm_left(ones, gated * gated, 2, NT)
        cross = mm_left(ones, gated * (gs_ref[k, 0] * gain[...]), 2, NT)
        sums_ref[0, 0, pl.ds(k, 1), :] = square[0:1]
        sums_ref[0, 1, pl.ds(k, 1), :] = cross[0:1]
        return carry

    lax.fori_loop(0, count, descend, 0)


def backward_kernel(
    heads, state, full_inner, prefix_ref, p_ref, gs_ref, xc_ref, bcc_ref, dt_ref, cum_ref, mixed_ref, sin_ref,
    rin_ref, tot_ref, cxw, cxb, cbw, cbb, dtb, nega, dsk, gain,
    g_ref, scaled_ref, small_ref, smallbc_ref, dm_scr, j_scr, h_scr, nx_scr, nb_scr, jrun_scr,
):
    count, _, span, _ = p_ref.shape
    width = cxw.shape[1]
    head_width = width // heads
    prefix = prefix_ref[pl.program_id(0)]
    lane = iota((span, width), 1)
    lane_head = lane // head_width
    expand = one_hot(iota((128, width), 0) == iota((128, width), 1) // head_width)
    pick = one_hot(iota((width, 128), 0) == iota((width, 128), 1) * head_width)
    same_head = one_hot(iota((width, width), 0) // head_width == iota((width, width), 1) // head_width)
    later = one_hot(iota((span, span), 1) >= iota((span, span), 0))
    row = iota((span, 1), 0)

    @pl.when(pl.program_id(0) == 0)
    def _():
        small_ref[...] = jnp.zeros_like(small_ref)
        smallbc_ref[...] = jnp.zeros_like(smallbc_ref)

    for ref in (h_scr, nx_scr, nb_scr, jrun_scr):
        ref[...] = jnp.zeros_like(ref)

    def ascend(k, carry):
        mean_sq = column(tot_ref[0, 0, pl.ds(k, 1), :]) * (1.0 / full_inner)
        mean_x = column(tot_ref[0, 1, pl.ds(k, 1), :]) * (1.0 / full_inner)
        scale = lax.rsqrt(mean_sq + EPSILON)
        gate = p_ref[k, 0, :, :width].astype(F32)
        sig = sigmoid(gate)
        act = gate * sig
        mixed = mixed_ref[k, 0]
        gated = mixed * act
        grad_scaled = gs_ref[k, 0]
        unit = gated * scale
        scaled_ref[k, 0] = (unit * gain[...]).astype(BF16)
        small_ref[5:6, :] += column_sum(grad_scaled * unit)
        dgated = grad_scaled * gain[...] * scale - unit * (scale * scale * mean_x)
        g_ref[k, 0, :, :width] = (dgated * mixed * (sig * (1.0 + gate * (1.0 - sig)))).astype(BF16)
        dm = dgated * act
        dm_scr[k] = dm
        cum = cum_ref[k, 0]
        end = cum[span - 1 :, :]
        cc = bcc_ref[k, 0, :, state:]
        c = cc * sigmoid(cc)
        jrun = jrun_scr[...]
        j_scr[k] = jrun
        jrun_scr[...] = jnp.exp(end) * jrun + mm(c, jnp.exp(end - cum) * dm, TN)
        return carry

    lax.fori_loop(0, count, ascend, 0)

    def descend(step, carry):
        k = count - 1 - step
        xc, bcc = xc_ref[k, 0], bcc_ref[k, 0]
        dt, cum, dm = dt_ref[k, 0], cum_ref[k, 0], dm_scr[k]
        xsig = sigmoid(xc)
        v = xc * xsig
        bsig = sigmoid(bcc)
        bc = bcc * bsig
        b, c = bc[:, :state].astype(BF16), bc[:, state:].astype(BF16)
        end = cum[span - 1 :, :]
        w = dt * v
        wb = w.astype(BF16)
        dmb = dm.astype(BF16)
        t, s, mask = chunk_masks(span, k, prefix)
        scores = jnp.where(mask, mm(c, b, NT), 0.0)
        side = jnp.where(t > s, 1.0, jnp.where(t < s, -1.0, 0.0))
        cum_t = cum.T
        dscore = jnp.zeros((span, span), F32)
        dw = jnp.zeros((span, width), F32)
        z = jnp.zeros((span, width), F32)
        for h in range(heads):
            at = h * head_width
            decay = jnp.exp(-jnp.abs(cum[:, at : at + 1] - cum_t[at : at + 1, :]))
            weight = scores * decay
            dm_h = jnp.where(lane_head == h, dmb, jnp.zeros_like(dmb))
            dweight = mm(dm_h, wb, NT)
            dw = dw + mm(weight, dm_h, TN)
            dscore = dscore + decay * dweight
            q = weight * dweight * side
            diff = jnp.sum(q - q.T, axis=1, keepdims=True)
            z = z + jnp.where(lane == at, diff, 0.0)
        dscore = jnp.where(mask, dscore, 0.0).astype(BF16)
        inside = row + k * span < prefix
        grow = jnp.exp(cum)
        fall = jnp.exp(end - cum)
        grow_in = jnp.where(inside, grow, 0.0)
        whole = jnp.exp(end)
        state_in, back_in = sin_ref[k, 0], rin_ref[k, 0]
        hgrad, jgrad = h_scr[...], j_scr[k]
        front = dm * grow
        rear = dm * fall
        wf = w * fall
        wg = w * grow_in
        bh, bj = mm(b, hgrad), mm(b, jgrad)
        out_b = rear * mm(c, back_in)
        src_f = wf * bh
        z = z + front * mm(c, state_in) - out_b - src_f + wg * bj
        edge = column_sum(out_b + src_f) + whole * column_sum(hgrad * state_in + jgrad * back_in)
        dw = dw + fall * bh + grow_in * bj
        dc = mm(dscore, b) + mm(front, state_in, NT) + mm(rear, back_in, NT)
        db = mm(dscore, c, TN) + mm(wf, hgrad, NT) + mm(wg, jgrad, NT)
        h_scr[...] = whole * hgrad + mm(c, front, TN)
        drate = mm_right(mm_left(later, z, 2) + edge, same_head, 2)
        raw = mm(p_ref[k, 0, :, 2 * width + 2 * state :], expand) + dtb[...]
        draw = (mm_right(v * dw, same_head, 2) + drate * nega[...]) * sigmoid(raw)
        small_ref[6:7, :] += column_sum(draw)
        small_ref[7:8, :] += column_sum(drate * (dt * nega[...]))
        small_ref[8:9, :] += column_sum(dm * v)
        g_ref[k, 0, :, 2 * width + 2 * state :] = mm(draw, pick).astype(BF16)
        dxc = (dt * dw + dsk[...] * dm) * (xsig * (1.0 + xc * (1.0 - xsig)))
        dbc = jnp.concatenate([db, dc], axis=1) * (bsig * (1.0 + bcc * (1.0 - bsig)))
        for grad, nref, sref, wref, lo, hi in (
            (dxc, nx_scr, small_ref, cxw, width, 2 * width),
            (dbc, nb_scr, smallbc_ref, cbw, 2 * width, 2 * width + 2 * state),
        ):
            win = conv_window(p_ref, k, lo, hi)
            for j in range(4):
                sref[j : j + 1, :] += column_sum(grad * taps(win, span, j))
            sref[4:5, :] += column_sum(grad)
            ext = jnp.concatenate([grad, nref[...]], axis=0)
            nref[...] = grad[:8]
            back = wref[3:4, :] * grad
            for j in range(3):
                back = back + wref[j : j + 1, :] * ext[3 - j : 3 - j + span]
            g_ref[k, 0, :, lo:hi] = back.astype(BF16)
        return carry

    lax.fori_loop(0, count, descend, 0)


def group_block(shape):
    return pl.BlockSpec((shape[0], 1) + tuple(shape[2:]), lambda g: (0, g, 0, 0))


def sums_block(count, span):
    return pl.BlockSpec((1, 2, count, span), lambda g: (g, 0, 0, 0))


def whole_block(a):
    return pl.BlockSpec(a.shape, lambda g: (0,) * a.ndim)


def ssd_forward(heads, state, prefix, p, gs, params):
    count, group, span, _ = p.shape
    width = params[0].shape[1]
    outs = [
        (count, group, span, width), (count, group, span, 2 * state), (count, group, span, width),
        (count, group, span, width), (count, group, span, width), (count, group, state, width),
        (count, group, state, width),
    ]
    return pl.pallas_call(
        functools.partial(forward_kernel, heads, state),
        grid=(group,),
        in_specs=[pl.BlockSpec(memory_space=pltpu.SMEM), group_block(p.shape), group_block(gs.shape)]
        + [whole_block(a) for a in params],
        out_specs=[group_block(o) for o in outs] + [sums_block(count, span)],
        out_shape=[jax.ShapeDtypeStruct(o, F32) for o in outs + [(group, 2, count, span)]],
        scratch_shapes=[pltpu.VMEM((state, width), F32)] * 2,
        compiler_params=pltpu.CompilerParams(vmem_limit_bytes=56 << 20),
    )(prefix, p, gs, *params)


def ssd_backward(heads, state, full_inner, prefix, p, gs, saved, totals, params):
    count, group, span, cols = p.shape
    width = params[0].shape[1]
    ins = (p, gs) + tuple(saved) + (totals,)
    return pl.pallas_call(
        functools.partial(backward_kernel, heads, state, full_inner),
        grid=(group,),
        in_specs=[pl.BlockSpec(memory_space=pltpu.SMEM)]
        + [group_block(a.shape) for a in ins[:-1]] + [sums_block(count, span)]
        + [whole_block(a) for a in params],
        out_specs=[
            group_block(p.shape), group_block((count, group, span, width)),
            pl.BlockSpec((16, width), lambda g: (0, 0)), pl.BlockSpec((8, 2 * state), lambda g: (0, 0)),
        ],
        out_shape=[
            jax.ShapeDtypeStruct(p.shape, BF16), jax.ShapeDtypeStruct((count, group, span, width), BF16),
            jax.ShapeDtypeStruct((16, width), F32), jax.ShapeDtypeStruct((8, 2 * state), F32),
        ],
        scratch_shapes=[
            pltpu.VMEM((count, span, width), F32), pltpu.VMEM((count, state, width), F32),
            pltpu.VMEM((state, width), F32), pltpu.VMEM((8, width), F32), pltpu.VMEM((8, 2 * state), F32),
            pltpu.VMEM((state, width), F32),
        ],
        compiler_params=pltpu.CompilerParams(vmem_limit_bytes=60 << 20),
    )(prefix, *ins, *params)


def ring_place(s, n):
    return (1 - s % 2) * (s // 2) + (s % 2) * (n - 1 - s // 2)


def ring_index(p, n):
    p = (p + 2 * n) % n
    far = p // (n // 2)
    return (1 - far) * 2 * p + far * (2 * (n - 1 - p) + 1)


def axes_here():
    return {a: (lax.axis_index(a), lax.axis_size(a)) for a in ("dp", "seq", "head")}


def greet(axis_names, diagonal=False):
    here = axes_here()
    barrier = pltpu.get_barrier_semaphore()
    total = 0
    for axis in axis_names:
        me, size = here[axis]
        total += size - 1

        def hello(k, carry, axis=axis, me=me, size=size):
            pl.semaphore_signal(
                barrier, inc=1, device_id={axis: (me + 1 + k) % size}, device_id_type=pl.DeviceIdType.MESH
            )
            return carry

        lax.fori_loop(0, size - 1, hello, 0)
    if diagonal:
        (me_dp, dp), (me, sq) = here["dp"], here["seq"]
        total += (dp - 1) * (sq - 1)

        def across(k, carry):
            for d in range(1, dp):
                pl.semaphore_signal(
                    barrier, inc=1, device_id={"dp": (me_dp + d) % dp, "seq": (me + 1 + k) % sq},
                    device_id_type=pl.DeviceIdType.MESH,
                )
            return carry

        lax.fori_loop(0, sq - 1, across, 0)
    pl.semaphore_wait(barrier, total)


def remote(src, dst, send, recv, axis, index):
    return pltpu.make_async_remote_copy(
        src_ref=src, dst_ref=dst, send_sem=send, recv_sem=recv,
        device_id=dict(zip(axis, index)) if isinstance(axis, tuple) else {axis: index}, device_id_type=pl.DeviceIdType.MESH,
    )


def gather_kernel(
    own_a, own_b, w3, wb, wd, all_a, all_b, w3_all, wb_all, wd_all,
    local, r_send, r_recv, l_send, l_recv, s_send, s_recv, q_send, q_recv, d_send, d_recv,
):
    here = axes_here()
    (me_dp, dp), (me, sq), (me_head, hd) = here["dp"], here["seq"], here["head"]
    place = ring_place(me, sq)
    right, left = ring_index(place + 1, sq), ring_index(place - 1, sq)
    other = hd - 1 - me_head
    half = sq // 2
    rows = own_a.shape[0]
    piece = rows // 2
    width = w3_all.shape[-1]
    greet(("dp", "seq", "head"))

    pairs = ((own_a, all_a), (own_b, all_b))
    own_copies = []
    for i, (own, out) in enumerate(pairs):
        own_copies.append(pltpu.make_async_copy(own, out.at[me, me_head], local.at[i]))
    mats = (
        (lambda s: w3.at[:, :, pl.ds(pl.multiple_of(s * width, width), width)], lambda d, s: w3_all.at[:, d, s]),
        (lambda s: wb, lambda d, s: wb_all.at[d, s]),
        (lambda s: wd.at[s], lambda d, s: wd_all.at[d, s]),
    )
    for i, (src, dst) in enumerate(mats):
        own_copies.append(pltpu.make_async_copy(src(me), dst(me_dp, me), local.at[2 + i]))
    for copy in own_copies:
        copy.start()

    def sub(ref, h):
        return ref.at[pl.ds(h * piece, piece)]

    def block(out, index, h):
        return sub(out.at[index, me_head], h)

    def to_sibling(i, slot, h, src, dst):
        remote(src, dst, s_send.at[i, slot, h], s_recv.at[i, slot, h], "head", other).start()

    for i, (own, out) in enumerate(pairs):
        for h in range(2):
            src, dst = sub(own, h), block(out, me, h)
            remote(src, dst, r_send.at[i, 0, h], r_recv.at[i, 0, h], "seq", right).start()
            remote(src, dst, l_send.at[i, 0, 1 - h], l_recv.at[i, 0, 1 - h], "seq", left).start()
        if i == 0:
            def scatter(k, carry):
                peer = (me + 1 + k) % sq
                for m, (src, dst) in enumerate(mats):
                    remote(src(peer), dst(me_dp, me), q_send.at[m, k], q_recv.at[m, k], "seq", peer).start()
                return carry

            lax.fori_loop(0, sq - 1, scatter, 0)

    for i, (own, out) in enumerate(pairs):
        for h in range(2):
            to_sibling(i, 0, h, sub(own, h), block(out, me, h))

    def forward(k, carry):
        source = (me + 2 * sq - 1 - k) % sq
        for d in range(1, dp):
            for m, (src, dst) in enumerate(mats):
                remote(
                    dst(me_dp, source), dst(me_dp, source), d_send.at[m, d - 1, k + 1], d_recv.at[m, d - 1, k + 1],
                    "dp", (me_dp + d) % dp,
                ).start()
        return carry

    for copy in own_copies[len(pairs):]:
        copy.wait()
    forward(-1, 0)

    def arrived(k, carry):
        source = (me + 2 * sq - 1 - k) % sq
        for m, (src, dst) in enumerate(mats):
            remote(
                src((me + 1 + k) % sq), dst(me_dp, source), q_send.at[m, k], q_recv.at[m, k],
                "seq", (me + 1 + k) % sq,
            ).wait()
        return forward(k, carry)

    for hop in range(1, half + 1):
        for i, (own, out) in enumerate(pairs):
            from_left = ring_index(place - hop, sq)
            from_right = ring_index(place + hop, sq)
            for h in range(2):
                if hop < half or h == 0:
                    ref = block(out, from_left, h)
                    remote(ref, ref, r_send.at[i, hop - 1, h], r_recv.at[i, hop - 1, h], "seq", right).wait_recv()
                    if hop < half - 1 or (hop == half - 1 and h == 0):
                        remote(ref, ref, r_send.at[i, hop, h], r_recv.at[i, hop, h], "seq", right).start()
                    to_sibling(i, hop, h, ref, ref)
                g = 1 - h
                if hop < half or g == 1:
                    ref = block(out, from_right, g)
                    remote(ref, ref, l_send.at[i, hop - 1, h], l_recv.at[i, hop - 1, h], "seq", left).wait_recv()
                    if hop < half - 1 or (hop == half - 1 and g == 1):
                        remote(ref, ref, l_send.at[i, hop, h], l_recv.at[i, hop, h], "seq", left).start()
                    if hop < half:
                        to_sibling(i, half + hop, g, ref, ref)
                    else:
                        to_sibling(i, half, 1, ref, ref)
        if hop == 1:
            lax.fori_loop(0, sq - 1, arrived, 0)

    for i, (own, out) in enumerate(pairs):
        for hop in range(half):
            for h in range(2):
                if hop < half - 1 or h == 0:
                    ref = block(out, me, h)
                    remote(ref, ref, r_send.at[i, hop, h], r_recv.at[i, hop, h], "seq", right).wait_send()
                    remote(ref, ref, l_send.at[i, hop, h], l_recv.at[i, hop, h], "seq", left).wait_send()
        for slot in range(sq):
            step = slot if slot <= half else half - slot
            source = ring_index(place - step, sq)
            for h in range(2):
                mine = block(out, source, h)
                theirs = sub(out.at[source, other], h)
                copy = remote(mine, theirs, s_send.at[i, slot, h], s_recv.at[i, slot, h], "head", other)
                copy.wait_send()
                copy.wait_recv()

    def last(k, carry):
        source = (me + 2 * sq - k) % sq
        for d in range(1, dp):
            came = (me_dp + dp - d) % dp
            for m, (src, dst) in enumerate(mats):
                copy = remote(
                    dst(me_dp, source), dst(came, source), d_send.at[m, d - 1, k], d_recv.at[m, d - 1, k],
                    "dp", (me_dp + d) % dp,
                )
                copy.wait_send()
                copy.wait_recv()
        return carry

    lax.fori_loop(0, sq, last, 0)
    for copy in own_copies[:len(pairs)]:
        copy.wait()


def gather_all(own_a, own_b, w3, wb, wd, collective_id=0):
    dp, sq, hd = lax.axis_size("dp"), lax.axis_size("seq"), lax.axis_size("head")
    rows, model = own_a.shape
    kinds, depth, half = w3.shape
    width = half // sq
    anywhere = pl.BlockSpec(memory_space=pl.ANY)
    dma = pltpu.SemaphoreType.DMA
    S = jax.ShapeDtypeStruct
    return pl.pallas_call(
        gather_kernel,
        out_shape=[
            S((sq, hd, rows, model), BF16), S((sq, hd, rows, model), BF16),
            S((kinds, dp, sq, depth, width), BF16), S((dp, sq) + wb.shape, BF16), S((dp, sq) + wd.shape[1:], BF16),
        ],
        in_specs=[anywhere] * 5,
        out_specs=[anywhere] * 5,
        scratch_shapes=[
            dma((5,)), dma((2, sq // 2, 2)), dma((2, sq // 2, 2)), dma((2, sq // 2, 2)), dma((2, sq // 2, 2)),
            dma((2, sq, 2)), dma((2, sq, 2)), dma((3, sq)), dma((3, sq)), dma((3, dp, sq)), dma((3, dp, sq)),
        ],
        compiler_params=pltpu.CompilerParams(collective_id=collective_id, has_side_effects=True),
    )(own_a, own_b, w3, wb, wd)


def scatter_kernel(
    parts, xs0, xs1, g3, gb, gd, small, sb,
    out0, out1, o3, ob, od, osmall, osb,
    own_x, sib_x, rbuf, lbuf, fin, v3, vb, vd, l3, lb, ld,
    local, x_send, x_recv, r_send, r_recv, l_send, l_recv, f_send, f_recv,
    d_send, d_recv, q_send, q_recv, b_send, b_recv,
):
    here = axes_here()
    (me_dp, dp), (me, sq), (me_head, hd) = here["dp"], here["seq"], here["head"]
    place = ring_place(me, sq)
    right, left = ring_index(place + 1, sq), ring_index(place - 1, sq)
    other = hd - 1 - me_head
    half = sq // 2
    rows = own_x.shape[2]
    piece = rows // parts
    width = v3.shape[-1]
    near = range(parts)
    first, second = range(parts // 2), range(parts // 2, parts)
    xs, outs = (xs0, xs1), (out0, out1)
    rings = range(2)
    greet(("dp", "seq", "head"), diagonal=True)

    def sub(ref, h):
        return ref.at[pl.ds(h * piece, piece)]

    order = [half]
    for step in range(half - 1, 0, -1):
        order += [step, -step]
    order.append(0)
    loads = []
    for i in rings:
        for slot, step in enumerate(order):
            s = ring_index(place + step, sq)
            remote(
                xs[i].at[s, other], sib_x.at[i, slot], x_send.at[i, slot], x_recv.at[i, slot], "head", other
            ).start()
            copy = pltpu.make_async_copy(xs[i].at[s, me_head], own_x.at[i, slot], local.at[i, slot])
            copy.start()
            loads.append(copy)

    def mine(k):
        return (me + 1 + k) % sq

    kinds = (
        (lambda d, s: g3.at[:, d, s], v3, l3),
        (lambda d, s: gb.at[d, s], vb, lb),
        (lambda d, s: gd.at[d, s], vd, ld),
    )

    def share(k, carry):
        s = mine(k)
        for m, (src, own, land) in enumerate(kinds):
            pltpu.make_async_copy(src(me_dp, s), own.at[k], local.at[2 + m, k]).start()
            for d in range(1, dp):
                peer = (me_dp + d) % dp
                remote(
                    src(peer, s), land.at[d - 1, k], d_send.at[m, d - 1, k], d_recv.at[m, d - 1, k], "dp", peer
                ).start()
        return carry

    lax.fori_loop(0, sq, share, 0)

    smalls = ((small, osmall), (sb, osb))

    def tell(k, carry):
        for d in range(dp):
            for m, (src, dst) in enumerate(smalls):
                remote(
                    src, dst.at[me_head, me_dp, me], b_send.at[m, d, k], b_recv.at[m, d, k], ("dp", "seq"),
                    ((me_dp + d) % dp, mine(k)),
                ).start()
        return carry

    lax.fori_loop(0, sq - 1, tell, 0)
    for d in range(1, dp):
        for m, (src, dst) in enumerate(smalls):
            remote(
                src, dst.at[me_head, me_dp, me], b_send.at[m, d, sq - 1], b_recv.at[m, d, sq - 1],
                ("dp", "seq"), ((me_dp + d) % dp, me),
            ).start()
    keep = [pltpu.make_async_copy(src, dst.at[me_head, me_dp, me], local.at[5, m]) for m, (src, dst) in enumerate(smalls)]
    for copy in keep:
        copy.start()

    def ready(i, slot):
        remote(
            xs[i].at[me, other], sib_x.at[i, slot], x_send.at[i, slot], x_recv.at[i, slot], "head", other
        ).wait_recv()
        loads[i * sq + slot].wait()

    def both(i, slot, h):
        at = pl.ds(h * piece, piece)
        return own_x[i, slot, at].astype(F32) + sib_x[i, slot, at].astype(F32)

    def hop(i, t, h, to_right, src):
        sends, recvs, buf, axis_at = (r_send, r_recv, rbuf, right) if to_right else (l_send, l_recv, lbuf, left)
        return remote(src, sub(buf.at[i, t], h), sends.at[i, t, h], recvs.at[i, t, h], "seq", axis_at)

    def start_fresh(i, slot, t, h, to_right):
        at = pl.ds(h * piece, piece)
        own_x[i, slot, at] = both(i, slot, h).astype(BF16)
        hop(i, t, h, to_right, sub(own_x.at[i, slot], h)).start()

    def pass_on(i, slot, t, h, to_right):
        buf = rbuf if to_right else lbuf
        at = pl.ds(h * piece, piece)
        hop(i, t - 1, h, to_right, sub(buf.at[i, t - 1], h)).wait_recv()
        buf[i, t - 1, at] = (buf[i, t - 1, at].astype(F32) + both(i, slot, h)).astype(BF16)
        hop(i, t, h, to_right, sub(buf.at[i, t - 1], h)).start()

    def give(k, carry):
        s = mine(k)
        for m, (src, own, land) in enumerate(kinds):
            pltpu.make_async_copy(src(me_dp, s), own.at[k], local.at[2 + m, k]).wait()
            total = own[k].astype(F32)
            for d in range(1, dp):
                peer = (me_dp + d) % dp
                remote(
                    src(peer, s), land.at[d - 1, k], d_send.at[m, d - 1, k], d_recv.at[m, d - 1, k], "dp", peer
                ).wait_recv()
                total = total + land[d - 1, k].astype(F32)
            own[k] = total.astype(BF16)
        return carry

    def lane(s):
        return pl.ds(pl.multiple_of(s * width, width), width)

    def home(k, m, s_to, s_from):
        src = (v3, vb, vd)[m].at[k]
        dst = (o3.at[:, :, lane(s_from)], ob.at[me_head, s_from], od.at[s_from])[m]
        return remote(src, dst, q_send.at[m, k], q_recv.at[m, k], "seq", s_to)

    def give_away(k, carry):
        give(k, carry)
        for m in range(3):
            home(k, m, mine(k), me).start()
        return carry

    def finish(i):
        slot = sq - 1
        ready(i, slot)
        for h in range(parts):
            at = pl.ds(h * piece, piece)
            for to_right in (True, False):
                buf = rbuf if to_right else lbuf
                hop(i, half - 1, h, to_right, sub(buf.at[i, half - 1], h)).wait_recv()
            total = both(i, slot, h) + rbuf[i, half - 1, at].astype(F32) + lbuf[i, half - 1, at].astype(F32)
            fin[i, at] = total.astype(BF16)
            dst = sub(outs[i].at[me_head], h)
            pltpu.make_async_copy(sub(fin.at[i], h), dst, local.at[6 + i, h]).start()
            remote(sub(fin.at[i], h), dst, f_send.at[i, h], f_recv.at[i, h], "head", other).start()

    for t in range(half + 1):
        for i in rings:
            if t == 0:
                ready(i, 0)
                for h in first:
                    start_fresh(i, 0, 0, h, True)
                for h in second:
                    start_fresh(i, 0, 0, h, False)
            elif t < half:
                ready(i, 2 * t - 1)
                ready(i, 2 * t)
                for h in range(parts):
                    for to_right, slot, early in ((True, 2 * t - 1, first), (False, 2 * t, second)):
                        if t == 1 and h not in early:
                            start_fresh(i, slot, t, h, to_right)
                        else:
                            pass_on(i, slot, t, h, to_right)
            else:
                finish(i)
        lax.fori_loop(t * (sq - 1) // (half + 1), (t + 1) * (sq - 1) // (half + 1), give_away, 0)
    give(sq - 1, 0)
    mine_home = [
        pltpu.make_async_copy((v3, vb, vd)[m].at[sq - 1], dst, local.at[2 + m, sq])
        for m, dst in enumerate((o3.at[:, :, lane(me)], ob.at[me_head, me], od.at[me]))
    ]
    for copy in mine_home:
        copy.start()

    def relay_bc(source, k):
        return remote(
            ob.at[me_head, source], ob.at[me_head, source], f_send.at[2, k], f_recv.at[2, k], "head", other
        )

    def relay_small(m, d, source, k):
        ref = smalls[m][1].at[me_head, d, source]
        return remote(ref, ref, b_send.at[2 + m, d, k], b_recv.at[2 + m, d, k], "head", other)

    for copy in keep + mine_home:
        copy.wait()
    relay_bc(me, sq - 1).start()
    for m in range(2):
        relay_small(m, me_dp, me, sq - 1).start()

    def came(k):
        return (me + 2 * sq - 1 - k) % sq

    def collect(k, carry):
        for m in range(3):
            home(k, m, mine(k), came(k)).wait()
        relay_bc(came(k), k).start()
        for d in range(dp):
            frm = (me_dp + dp - d) % dp
            for m, (src, dst) in enumerate(smalls):
                remote(
                    src, dst.at[me_head, frm, came(k)], b_send.at[m, d, k], b_recv.at[m, d, k], ("dp", "seq"),
                    ((me_dp + d) % dp, mine(k)),
                ).wait()
                relay_small(m, frm, came(k), k).start()
        return carry

    lax.fori_loop(0, sq - 1, collect, 0)
    for d in range(1, dp):
        frm = (me_dp + dp - d) % dp
        for m, (src, dst) in enumerate(smalls):
            remote(
                src, dst.at[me_head, frm, me], b_send.at[m, d, sq - 1], b_recv.at[m, d, sq - 1], ("dp", "seq"),
                ((me_dp + d) % dp, me),
            ).wait()
            relay_small(m, frm, me, sq - 1).start()

    def settle(k, carry):
        relay_bc(came(k), k).wait_send()
        remote(
            ob.at[me_head, came(k)], ob.at[other, came(k)], f_send.at[2, k], f_recv.at[2, k], "head", other
        ).wait_recv()
        for d in range(dp):
            for m in range(2):
                relay_small(m, d, came(k), k).wait_send()
                ref = smalls[m][1].at[other, d, came(k)]
                remote(ref, ref, b_send.at[2 + m, d, k], b_recv.at[2 + m, d, k], "head", other).wait_recv()
        for m, (src, own, land) in enumerate(kinds):
            for d in range(1, dp):
                peer = (me_dp + d) % dp
                remote(
                    src(peer, mine(k)), land.at[d - 1, k], d_send.at[m, d - 1, k], d_recv.at[m, d - 1, k], "dp", peer
                ).wait_send()
        return carry

    lax.fori_loop(0, sq, settle, 0)
    for i in rings:
        for slot in range(sq):
            remote(
                xs[i].at[me, other], sib_x.at[i, slot], x_send.at[i, slot], x_recv.at[i, slot], "head", other
            ).wait_send()
        for t in range(half):
            for h in range(parts):
                for to_right, early in ((True, first), (False, second)):
                    if t > 0 or h in early:
                        hop(i, t, h, to_right, sub(own_x.at[i, 0], h)).wait_send()
        for h in range(parts):
            src = sub(fin.at[i], h)
            pltpu.make_async_copy(src, sub(outs[i].at[me_head], h), local.at[6 + i, h]).wait()
            copy = remote(src, sub(outs[i].at[other], h), f_send.at[i, h], f_recv.at[i, h], "head", other)
            copy.wait_send()
            copy.wait_recv()


def scatter_all(x0, x1, g3, gb, gd, small, sb, collective_id=1, parts=2):
    dp, sq, hd = lax.axis_size("dp"), lax.axis_size("seq"), lax.axis_size("head")
    _, _, rows, model = x0.shape
    kinds, _, _, depth, width = g3.shape
    anywhere = pl.BlockSpec(memory_space=pl.ANY)
    dma = pltpu.SemaphoreType.DMA
    S = jax.ShapeDtypeStruct
    V = pltpu.VMEM
    half = sq // 2
    return pl.pallas_call(
        functools.partial(scatter_kernel, parts),
        out_shape=[
            S((hd, rows, model), BF16), S((hd, rows, model), BF16), S((kinds, depth, sq * width), BF16),
            S((hd, sq) + gb.shape[2:], BF16), S((sq,) + gd.shape[2:], BF16),
            S((hd, dp, sq) + small.shape, F32), S((hd, dp, sq) + sb.shape, F32),
        ],
        in_specs=[anywhere] * 7,
        out_specs=[anywhere] * 7,
        scratch_shapes=[
            V((2, sq, rows, model), BF16), V((2, sq, rows, model), BF16),
            V((2, half, rows, model), BF16), V((2, half, rows, model), BF16), V((2, rows, model), BF16),
            V((sq, kinds, depth, width), BF16), V((sq,) + gb.shape[2:], BF16), V((sq,) + gd.shape[2:], BF16),
            V((dp - 1, sq, kinds, depth, width), BF16), V((dp - 1, sq) + gb.shape[2:], BF16),
            V((dp - 1, sq) + gd.shape[2:], BF16),
            dma((8, sq + 1)), dma((2, sq)), dma((2, sq)),
            dma((2, half, parts)), dma((2, half, parts)), dma((2, half, parts)), dma((2, half, parts)),
            dma((3, max(parts, sq))), dma((3, max(parts, sq))),
            dma((3, dp, sq)), dma((3, dp, sq)), dma((3, sq)), dma((3, sq)), dma((4, dp, sq)), dma((4, dp, sq)),
        ],
        compiler_params=pltpu.CompilerParams(
            collective_id=collective_id, has_side_effects=True, vmem_limit_bytes=56 << 20
        ),
    )(x0, x1, g3, gb, gd, small, sb)


def total_kernel(x, o, land, send, recv):
    here = axes_here()
    (me, sq), (me_head, hd) = here["seq"], here["head"]
    barrier = pltpu.get_barrier_semaphore()
    count = sq * hd
    flat = me * hd + me_head

    def peer(k):
        to = (flat + 1 + k) % count
        return {"seq": to // hd, "head": to % hd}

    def hello(k, carry):
        pl.semaphore_signal(barrier, inc=1, device_id=peer(k), device_id_type=pl.DeviceIdType.MESH)
        return carry

    lax.fori_loop(0, count - 1, hello, 0)
    pl.semaphore_wait(barrier, count - 1)

    def copy(k):
        return pltpu.make_async_remote_copy(
            src_ref=x, dst_ref=land.at[k], send_sem=send.at[k], recv_sem=recv.at[k],
            device_id=peer(k), device_id_type=pl.DeviceIdType.MESH,
        )

    def start(k, carry):
        copy(k).start()
        return carry

    lax.fori_loop(0, count - 1, start, 0)
    o[...] = x[...]

    def take(k, carry):
        copy(k).wait()
        o[...] += land[k]
        return carry

    lax.fori_loop(0, count - 1, take, 0)


def total_over_heads(x, collective_id):
    count = lax.axis_size("seq") * lax.axis_size("head")
    vmem = pl.BlockSpec(memory_space=pltpu.VMEM)
    dma = pltpu.SemaphoreType.DMA
    return pl.pallas_call(
        total_kernel,
        out_shape=jax.ShapeDtypeStruct(x.shape, x.dtype),
        in_specs=[vmem],
        out_specs=vmem,
        scratch_shapes=[pltpu.VMEM((count - 1,) + x.shape, x.dtype), dma((count - 1,)), dma((count - 1,))],
        compiler_params=pltpu.CompilerParams(collective_id=collective_id, has_side_effects=True),
    )(x)


def project_kernel(normed, cot, w3, wb, wd, p_ref, gs_ref):
    width = w3.shape[2]
    at = 0
    for weight in (w3.at[0], w3.at[1], wb, wd):
        cols = weight.shape[1]
        p_ref[:, at : at + cols] = mm(normed[...], weight[...]).astype(BF16)
        at += cols
    gs_ref[...] = mm(cot[...], w3[2])


def project(normed, cot, w3, wb, wd):
    rows, model = normed.shape
    width, tile = w3.shape[2], 256
    cols = 2 * width + wb.shape[1] + wd.shape[1]
    row_block = lambda n: pl.BlockSpec((tile, n), lambda i: (i, 0))
    return pl.pallas_call(
        project_kernel,
        grid=(rows // tile,),
        in_specs=[row_block(model), row_block(model)] + [whole_block(a) for a in (w3, wb, wd)],
        out_specs=[row_block(cols), row_block(width)],
        out_shape=[jax.ShapeDtypeStruct((rows, cols), BF16), jax.ShapeDtypeStruct((rows, width), F32)],
        compiler_params=pltpu.CompilerParams(vmem_limit_bytes=56 << 20),
    )(normed, cot, w3, wb, wd)


def product_kernel(normed, cot, g, scaled, w3, wb, wd, branch, gn, g3, gb, gd, gnorm):
    width = w3.shape[2]
    n, c = normed[...], cot[...]
    branch[...] = mm(scaled[...], w3[2], NT).astype(BF16)
    g3[2] = mm(c, scaled[...], TN).astype(BF16)
    at = 0
    total = jnp.zeros(gn.shape, F32)
    dots = jnp.zeros(gnorm.shape, F32)
    for i, weight in enumerate((w3.at[0], w3.at[1], wb, wd)):
        cols = weight.shape[1]
        part = g[:, at : at + cols]
        at += cols
        total = total + mm(part, weight[...], NT)
        if i < 3:
            grad = mm(n, part, TN)
            if i < 2:
                g3[i] = grad.astype(BF16)
            else:
                gb[...] = grad.astype(BF16)
            dots = dots + mm_left(jnp.ones((8, cols), BF16), grad * weight[...].astype(F32), 2, NT)
        else:
            grad = mm(part, n, TN)
            gd[...] = grad[:16].astype(BF16)
            dots = dots + jnp.sum(grad * weight[...].astype(F32).T, axis=0, keepdims=True)
    gn[...] = total.astype(BF16)
    gnorm[...] = dots


def products(normed, cot, g, scaled, w3, wb, wd):
    rows, model = normed.shape
    width, tile = w3.shape[2], 256
    col_block = lambda n: pl.BlockSpec((n, tile), lambda j: (0, j))
    row_block = lambda n: pl.BlockSpec((tile, n), lambda j: (j, 0))
    three = pl.BlockSpec((3, tile, width), lambda j: (0, j, 0))
    S = jax.ShapeDtypeStruct
    return pl.pallas_call(
        product_kernel,
        grid=(model // tile,),
        in_specs=[col_block(rows), col_block(rows), whole_block(g), whole_block(scaled), three,
                  row_block(wb.shape[1]), row_block(wd.shape[1])],
        out_specs=[col_block(rows), col_block(rows), three, row_block(wb.shape[1]), col_block(16), col_block(8)],
        out_shape=[
            S((rows, model), BF16), S((rows, model), BF16), S(w3.shape, BF16), S(wb.shape, BF16),
            S((16, model), BF16), S((8, model), F32),
        ],
        compiler_params=pltpu.CompilerParams(vmem_limit_bytes=60 << 20),
    )(normed, cot, g, scaled, w3, wb, wd)


def rms(x, gain):
    return x * lax.rsqrt(jnp.mean(x * x, axis=-1, keepdims=True) + EPSILON) * gain


def body(
    tokens, norm_gain, w_gate_in, w_x_in, w_bc_in, w_dt_in, conv_x_w, conv_x_b, conv_bc_w, conv_bc_b,
    dt_bias, a_log, d_skip, gate_gain, w_out, prefix_len, cotangent,
):
    dp, sq, hd = lax.axis_size("dp"), lax.axis_size("seq"), lax.axis_size("head")
    me_seq, me_head = lax.axis_index("seq"), lax.axis_index("head")
    micro, seqs, span, model = tokens.shape
    group = micro * seqs
    rows_here = group * span
    own_rows = rows_here // hd
    depth, half = w_x_in.shape
    width = half // sq
    heads = w_dt_in.shape[1] // sq
    state = w_bc_in.shape[1] // 2
    full_inner = half * hd
    prefix = prefix_len.reshape(group)

    def mine(x):
        return lax.dynamic_slice_in_dim(x.reshape(rows_here, model), me_head * own_rows, own_rows, 0)

    def blocks(x):
        return x.reshape(sq, group, span, -1)

    w3 = jnp.stack([w_gate_in, w_x_in, w_out.T])
    wd = jnp.pad(w_dt_in.T.reshape(sq, heads, depth), ((0, 0), (0, 16 - heads), (0, 0)))
    normed_own = rms(mine(tokens).astype(F32), norm_gain).astype(BF16)
    normed, cot, w3, wb, wd = gather_all(normed_own, mine(cotangent), w3, w_bc_in, wd, 0)
    normed = normed.reshape(sq * rows_here, model)
    cot = cot.reshape(sq * rows_here, model)
    w3 = w3.reshape(3, model, width)
    wb = wb.reshape(model, 2 * state)
    wd = jnp.pad(wd.transpose(0, 1, 3, 2).reshape(model, 16), ((0, 0), (0, 112)))

    def part(x, size, axis):
        return lax.dynamic_slice_in_dim(x, me_seq * size, size, axis)

    def spread(x):
        return jnp.repeat(part(x, heads, 0), width // heads)[None]

    params = (
        part(conv_x_w, width, 1), part(conv_x_b, width, 0)[None], conv_bc_w, conv_bc_b[None],
        spread(dt_bias), spread(-jnp.exp(a_log)), spread(d_skip), part(gate_gain, width, 0)[None],
    )
    p, gs = (blocks(a) for a in project(normed, cot, w3, wb, wd))
    *saved, sums = ssd_forward(heads, state, prefix, p, gs, params)
    totals = total_over_heads(sums, 1)
    g, scaled, small, smallbc = ssd_backward(heads, state, full_inner, prefix, p, gs, saved, totals, params)
    branch, gn, g3, gb, gd, gnorm = products(
        normed, cot, g.reshape(sq * rows_here, -1), scaled.reshape(sq * rows_here, width), w3, wb, wd
    )
    by_head = small[6:9].reshape(3, heads, width // heads)
    per_head = jnp.concatenate([by_head[:2, :, 0], jnp.sum(by_head[2:], axis=2)], axis=0).reshape(1, 3 * heads)
    small = jnp.concatenate(
        [small[:6], jnp.pad(per_head, ((0, 0), (0, width - 3 * heads))), jnp.zeros((1, width), F32)], axis=0
    )
    wide = jnp.concatenate([smallbc, (gnorm[0] / norm_gain).reshape(8, model // 8)], axis=0)
    to_own = lambda x: x.reshape(sq, hd, own_rows, model)
    branch, gn, o3, ob, od, small, wide = scatter_all(
        to_own(branch), to_own(gn), g3.reshape(3, dp, sq, depth, width), gb.reshape(dp, sq, depth, 2 * state),
        gd.reshape(16, dp, sq, depth).transpose(1, 2, 0, 3), small, wide, 2,
    )

    def natural(x):
        return x.reshape(tokens.shape)

    x = tokens.astype(F32)
    result = (x + natural(branch).astype(F32)).astype(BF16)
    _, pull_norm = jax.vjp(lambda v: rms(v, norm_gain), x)
    grad_tokens = cotangent.astype(F32) + pull_norm(natural(gn).astype(F32))[0]
    o3 = o3.astype(F32)
    g_bc = jnp.sum(ob.astype(F32), axis=(0, 1))
    g_dt = od[:, :heads].transpose(2, 0, 1).reshape(depth, sq * heads).astype(F32)
    small = jnp.sum(lax.dynamic_index_in_dim(small, me_head, 0, False), axis=0)
    wide = jnp.sum(wide, axis=(0, 1, 2))
    lanes = lambda a: a.swapaxes(0, 1).reshape(a.shape[1], half)
    g_channel = lanes(small)
    g_head = small[:, 6, : 3 * heads].reshape(sq, 3, heads).swapaxes(0, 1).reshape(3, sq * heads)
    return (
        result, grad_tokens, wide[8:].reshape(model), o3[0], o3[1], g_bc, g_dt,
        g_channel[:4], g_channel[4], wide[:4], wide[4], g_head[0], g_head[1], g_head[2], g_channel[5], o3[2].T,
    )


def solution(mesh):
    rows = P(("dp", "seq"), "head")
    tok = P(None, "dp", "seq", None)
    return jax.shard_map(
        body,
        mesh=mesh,
        in_specs=(
            tok, P(), rows, rows, P(("dp", "seq"), None), rows, P(None, "head"), P("head"), P(), P(),
            P("head"), P("head"), P("head"), P("head"), P("head", ("dp", "seq")), P(None, "dp"), tok,
        ),
        out_specs=(
            tok, tok, P(), rows, rows, P(("dp", "seq"), None), rows, P(None, "head"), P("head"), P(), P(),
            P("head"), P("head"), P("head"), P("head"), P("head", ("dp", "seq")),
        ),
        check_vma=False,
    )
```
